32 devices in a mesh: ckpt: 1, vocab: 32 (over z, y, x, core).
Axes of the slice: x: 2, y: 2, z: 4, core: 2. Of those that a mesh axis runs over, the one named last changes fastest.
Arguments:
- hidden: bfloat16 [1, 512, 2048], P('ckpt', 'vocab'), may hold values from -16 to 16
- head: bfloat16 [1, 2048, 65536], P('ckpt', None, 'vocab'), may hold values from -1 to 1
- targets: int32 [512], replicated, may hold values from 0 to 65535
- segments: int32 [512], replicated, may hold values from 0 to 15, never falling along the last dimension, each value on 1 to 64 neighbouring positions
Outputs:
- scores: float32 [16], replicated
The draws below stay inside these ranges and needn't reach their ends.
All inputs are finite; a program needn't handle non-finite values.
Results may differ from the reference program's by a relative error of at most 0.0003.
Values may be sent and summed in bfloat16 or wider, within the bound.
No kernel may reach another device: no remote copies, remote signals or barrier semaphores. Data moves between devices by JAX's collectives and lax.ppermute only.
A program may use at most 64 MiB of HBM per device.

```python
import math
import jax
import jax.numpy as jnp
import numpy as np
from jax import lax

D = 2048
SEQ_MOST = 64
CKPTS = 1
VOCAB = 65536
TOKENS = 512
SEQS = 16


def make_head(key):
    weights = jax.random.normal(jax.random.fold_in(key, 11), (CKPTS, D, VOCAB), jnp.float32)
    weights = jnp.clip(weights * (3.0 / jnp.sqrt(1.0 * D)), -0.9, 0.9)
    return weights


def make_targets(key):
    wanted = jax.random.randint(jax.random.fold_in(key, 31), (TOKENS,), 0, VOCAB, jnp.int32)
    wanted = wanted.at[0].set(0)
    return wanted.at[TOKENS - 1].set(VOCAB - 1)


def draw_head(key, part):
    return make_head(key).astype(jnp.bfloat16)


def draw_targets(key, part):
    return make_targets(key)


def draw_hidden(key, part):
    states = jax.random.normal(jax.random.fold_in(key, 21), (CKPTS, TOKENS, D), jnp.float32)
    states = jnp.clip(states, -6.0, 6.0)
    weights = make_head(key).astype(jnp.bfloat16).astype(jnp.float32)
    wanted = make_targets(key)
    columns = jnp.transpose(jnp.take(weights, wanted, axis=2), (0, 2, 1))
    lengths = jnp.sum(columns * columns, axis=2, keepdims=True)
    chosen = (jax.random.randint(jax.random.fold_in(key, 32), (CKPTS, TOKENS, 1), 0, 3) == 0).astype(jnp.float32)
    lift = jax.random.uniform(jax.random.fold_in(key, 33), (CKPTS, TOKENS, 1), jnp.float32, 8.0, 22.0)
    aligned = chosen * lift * columns / lengths
    states = jnp.clip(states + aligned, -16.0, 16.0)
    return states.astype(jnp.bfloat16)


def length_profile(amount, total, reach, skew):
    portions = [(1 << 20) // math.isqrt(standing ** skew) + 1 for standing in range(2, amount + 1)]
    rest, holding = total - reach - (amount - 1), [1] * (amount - 1)
    while rest > 0:
        movable = [i for i in range(amount - 1) if holding[i] < reach]
        pool, budget = sum([portions[i] for i in movable]), rest
        for i in movable:
            extra = min(reach - holding[i], max(1, budget * portions[i] // pool), rest)
            holding[i] = holding[i] + extra
            rest = rest - extra
    return np.array([reach] + holding)


def uneven_parts(stream_key, amount, total, limit, lean):
    if amount == 2:
        one = jax.random.randint(stream_key, (), max(1, total - limit), min(limit, total - 1) + 1)
        return jnp.stack([one, total - one])
    sizes = jnp.asarray(length_profile(amount, total, limit, lean), jnp.int32)
    pairs = (amount - 1) // 2
    source_of, sink = sizes[1:1 + 2 * pairs:2], sizes[2:2 + 2 * pairs:2]
    margin = jnp.minimum(source_of - 1, limit - sink)
    shifted = jax.random.randint(jax.random.fold_in(stream_key, 1), (pairs,), 0, 1 << 20) % (margin + 1)
    sizes = sizes.at[1:1 + 2 * pairs:2].set(source_of - shifted).at[2:2 + 2 * pairs:2].set(sink + shifted)
    return sizes[jax.random.permutation(jax.random.fold_in(stream_key, 2), amount)]


def setup_inputs(seed: int = 0) -> dict:
    key_list = jax.random.split(jax.random.key(seed), 5)
    hidden = draw_hidden(jax.random.fold_in(key_list[4], 71), 0)
    head = draw_head(jax.random.fold_in(key_list[4], 71), 0)
    targets = draw_targets(jax.random.fold_in(key_list[4], 71), 0)
    segments = jnp.searchsorted(jnp.cumsum(uneven_parts(key_list[3], SEQS, TOKENS, SEQ_MOST, 0)), jnp.arange(TOKENS), side="right").astype(jnp.int32)
    return dict(hidden=hidden, head=head, targets=targets, segments=segments)


def checkpoint_errors(hidden_one, head_one, targets):
    block = min(512, TOKENS)
    row_blocks = hidden_one.reshape(TOKENS // block, block, D)
    wanted_blocks = targets.reshape(TOKENS // block, block)

    def one_block(pair):
        rows_block, wanted = pair
        logits = jnp.dot(rows_block, head_one, preferred_element_type=jnp.float32)
        probs = jax.nn.softmax(logits, axis=1)
        onehot = (jnp.arange(VOCAB, dtype=jnp.int32)[None, :] == wanted[:, None]).astype(jnp.float32)
        return jnp.sqrt(lax.optimization_barrier(jnp.sum((probs - onehot) ** 2, axis=1)))
    return lax.map(one_block, (row_blocks, wanted_blocks)).reshape(TOKENS)

def reference(hidden, head, targets, segments):
    onehot = (jnp.arange(SEQS, dtype=jnp.int32)[:, None] == segments[None, :]).astype(jnp.float32)
    counts = lax.optimization_barrier(jnp.sum(onehot, axis=1))
    total = jnp.zeros((SEQS,), jnp.float32)
    for index in range(CKPTS):
        errors = checkpoint_errors(hidden[index], head[index], targets)
        total = total + jnp.dot(onehot, errors, precision=lax.Precision.HIGHEST) / counts
    return total
```

```python
import functools

import jax
import jax.numpy as jnp
from jax import lax
from jax.experimental import pallas as pl
from jax.experimental.pallas import tpu as pltpu
from jax.sharding import PartitionSpec as P

LANES = 128
STEP = 256
VMEM = pl.BlockSpec(memory_space=pltpu.VMEM)
SMEM = pl.BlockSpec(memory_space=pltpu.SMEM)
HBM = pl.BlockSpec(memory_space=pltpu.HBM)


def columns_of(order, me, wanted_ref, per, width, start, rows):
    blocks = [
        wanted_ref[pl.ds(pl.multiple_of((me ^ order[b]) * per, per), per), :]
        for b in range(start // per, (start + rows) // per)
    ]
    return jnp.concatenate(blocks, axis=0) - me * width


def row_stats(order, me, rows_ref, head_ref, wanted_ref, logits_ref, store, arrive=None):
    width = head_ref.shape[1]
    count = rows_ref.shape[0]
    per = count // len(order)
    largest = None
    for left in range(0, width, STEP):
        if arrive is not None:
            arrive(left // STEP)
        logits = jnp.dot(
            rows_ref[...], head_ref[:, pl.ds(left, STEP)], preferred_element_type=jnp.float32
        )
        logits_ref[:, pl.ds(left, STEP)] = logits
        for j in range(0, STEP, LANES):
            part = logits[:, j : j + LANES]
            largest = part if largest is None else jnp.maximum(largest, part)
    tops = jnp.max(largest, axis=1, keepdims=True)
    chunk = min(64, count)
    lane = lax.broadcasted_iota(jnp.int32, (chunk, LANES), 1)
    for start in range(0, count, chunk):
        rows = pl.ds(start, chunk)
        top = tops[start : start + chunk]
        column = columns_of(order, me, wanted_ref, per, width, start, chunk)
        total = jnp.zeros((chunk, LANES), jnp.float32)
        squares = jnp.zeros((chunk, LANES), jnp.float32)
        target = jnp.zeros((chunk, LANES), jnp.float32)
        for left in range(0, width, LANES):
            part = logits_ref[rows, pl.ds(left, LANES)]
            expo = jnp.exp(part - top)
            hit = lane == column - left
            total += expo
            squares += jnp.where(hit, 0.0, expo * expo)
            target += jnp.where(hit, part, 0.0)
        total = jnp.sum(total, axis=1, keepdims=True)
        squares = jnp.sum(squares, axis=1, keepdims=True)
        target = jnp.sum(target, axis=1, keepdims=True)
        packed = jnp.where(
            lane == 0, top, jnp.where(lane == 1, total, jnp.where(lane == 2, squares, target))
        )
        store(start, packed)


def first_kernel(order, me_ref, rows_ref, source_ref, wanted_ref, out_ref, head_ref, logits_ref, sems):
    def copy(tile):
        columns = pl.ds(tile * STEP, STEP)
        return pltpu.make_async_copy(source_ref.at[:, columns], head_ref.at[:, columns], sems.at[tile])

    for tile in range(head_ref.shape[1] // STEP):
        copy(tile).start()

    def store(start, packed):
        out_ref[pl.ds(start, packed.shape[0]), :] = packed

    row_stats(
        order, me_ref[0], rows_ref, head_ref, wanted_ref, logits_ref, store, lambda tile: copy(tile).wait()
    )


def middle_kernel(order, me_ref, rows_ref, head_ref, wanted_ref, out_ref, logits_ref):
    def store(start, packed):
        out_ref[pl.ds(start, packed.shape[0]), :] = packed

    row_stats(order, me_ref[0], rows_ref, head_ref, wanted_ref, logits_ref, store)


def last_kernel(
    order, first, middle, me_ref, rows_ref, head_ref, wanted_ref, first_ref, middle_ref, out_ref, logits_ref, placed_ref
):
    me = me_ref[0]
    per = rows_ref.shape[0] // len(order)

    def place(device, value):
        placed_ref[pl.ds(pl.multiple_of((me ^ device) * per, per), per), :] = value

    for devices, ref in ((first, first_ref), (middle, middle_ref)):
        for b, device in enumerate(devices):
            place(device, ref[pl.ds(b * per, per), :])

    def store(start, packed):
        for at in range(0, packed.shape[0], per):
            place(order[(start + at) // per], packed[at : at + per])

    row_stats(order, me, rows_ref, head_ref, wanted_ref, logits_ref, store)
    for start in range(0, placed_ref.shape[0], LANES):
        turned = jnp.transpose(placed_ref[pl.ds(start, LANES), :])
        out_ref[:, pl.ds(start, LANES)] = turned[:4]


def merge(mine, other):
    top = jnp.maximum(mine[0:1], other[0:1])
    scale = jnp.exp(mine[0:1] - top)
    other_scale = jnp.exp(other[0:1] - top)
    total = mine[1:2] * scale + other[1:2] * other_scale
    squares = mine[2:3] * (scale * scale) + other[2:3] * (other_scale * other_scale)
    return top, total, squares, mine[3:4] + other[3:4]


def merge_kernel(mine_ref, other_ref, out_ref):
    out_ref[...] = jnp.concatenate(merge(mine_ref[...], other_ref[...]), axis=0)


def final_kernel(mine_ref, other_ref, segments_ref, out_ref):
    top, total, squares, target = merge(mine_ref[...], other_ref[...])
    prob = jnp.exp(target - top) / total
    errors = jnp.sqrt((1.0 - prob) ** 2 + squares / (total * total))
    count = out_ref.shape[1]
    tokens = errors.shape[1]
    member = lax.broadcasted_iota(jnp.int32, (count, tokens), 0) == segments_ref[...]
    sums = jnp.sum(jnp.where(member, errors, 0.0), axis=1, keepdims=True)
    counts = jnp.sum(jnp.where(member, 1.0, 0.0), axis=1, keepdims=True)
    means = sums / counts
    diagonal = lax.broadcasted_iota(jnp.int32, (count, count), 0) == lax.broadcasted_iota(
        jnp.int32, (count, count), 1
    )
    out_ref[...] = jnp.sum(jnp.where(diagonal, means, 0.0), axis=0, keepdims=True)


def on_device(devices, hidden, head, targets, segments):
    def exchange(x, mask):
        return lax.ppermute(x, "vocab", [(i, i ^ mask) for i in range(devices)])

    rows, weights = hidden[0], head[0]
    per, depth = rows.shape
    width = weights.shape[1]
    tokens = per * devices
    me = lax.axis_index("vocab").astype(jnp.int32).reshape(1)
    wanted = jnp.broadcast_to(targets[:, None], (tokens, LANES))
    weights = pltpu.with_memory_space_constraint(weights, pltpu.HBM)

    def statistics(kernel, order, count, out_shape, scratch, *arrays):
        room = 4 * count * width + 2 * count * depth + 12 * tokens * LANES + (4 << 20)
        return pl.pallas_call(
            functools.partial(kernel, *order),
            out_shape=out_shape,
            in_specs=[SMEM] + [HBM if a is weights else VMEM for a in arrays],
            out_specs=jax.tree.map(lambda _: VMEM, out_shape),
            scratch_shapes=[pltpu.VMEM((count, width), jnp.float32)] + scratch,
            compiler_params=pltpu.CompilerParams(
                vmem_limit_bytes=room + (2 * depth * width if kernel is first_kernel else 0)
            ),
            cost_estimate=pl.CostEstimate(
                flops=2 * count * depth * width,
                bytes_accessed=2 * (count * depth + depth * width),
                transcendentals=count * width,
            ),
        )(me, *arrays)

    pieces, order, first = [rows], [0], None
    bit = devices // 2
    while bit > 1:
        masks = [bit // 2, bit, bit + bit // 2] if bit > 2 else [bit]
        rows = jnp.concatenate(pieces, axis=0)
        pieces = pieces + [exchange(rows, m) for m in masks]
        order = order + [m ^ o for m in masks for o in order]
        if first is None:
            first = tuple(order)
            pieces = [jnp.concatenate(pieces, axis=0)]
            first_other = exchange(pieces[0], 1)
            count = len(first) * per
            early, resident = statistics(
                first_kernel,
                (first,),
                count,
                (jax.ShapeDtypeStruct((count, LANES), jnp.float32), pltpu.VMEM(weights.shape, weights.dtype)),
                [pltpu.SemaphoreType.DMA((width // STEP,))],
                pieces[0],
                weights,
                wanted,
            )
        bit //= len(masks) + 1
    pieces, early, first_other = lax.optimization_barrier((pieces, early, first_other))
    middle_rows = jnp.concatenate(pieces[1:], axis=0)
    middle = tuple(order[len(first) :])
    middle_other = exchange(middle_rows, 1)
    count = len(middle) * per
    between = statistics(
        middle_kernel,
        (middle,),
        count,
        jax.ShapeDtypeStruct((count, LANES), jnp.float32),
        [],
        middle_rows,
        resident,
        wanted,
    )
    last = tuple(1 ^ o for o in first + middle)
    stats = statistics(
        last_kernel,
        (last, first, middle),
        len(last) * per,
        jax.ShapeDtypeStruct((4, tokens), jnp.float32),
        [pltpu.VMEM((tokens, LANES), jnp.float32)],
        jnp.concatenate([first_other, middle_other], axis=0),
        resident,
        wanted,
        early,
        between,
    )

    small = pltpu.CompilerParams(vmem_limit_bytes=2 << 20)
    masks = [1]
    while 2 * (masks[-1] & ~1 or 1) < devices:
        masks.append(2 * (masks[-1] & ~1 or 1) | 1)
    for mask in masks[:-1]:
        stats = pl.pallas_call(
            merge_kernel,
            out_shape=jax.ShapeDtypeStruct(stats.shape, jnp.float32),
            in_specs=[VMEM, VMEM],
            out_specs=VMEM,
            compiler_params=small,
        )(stats, exchange(stats, mask))
    means = pl.pallas_call(
        final_kernel,
        out_shape=jax.ShapeDtypeStruct((1, tokens // 32), jnp.float32),
        in_specs=[VMEM, VMEM, VMEM],
        out_specs=VMEM,
        compiler_params=small,
    )(stats, exchange(stats, masks[-1]), segments[None, :])
    return lax.psum(means[0], "ckpt")


def solution(mesh):
    placed = (P("ckpt", "vocab", None), P("ckpt", None, "vocab"), P(), P())
    body = functools.partial(on_device, mesh.shape["vocab"])
    return jax.shard_map(body, mesh=mesh, in_specs=placed, out_specs=P(), check_vma=False)
```
